256 devices in a mesh: sector: 8 (over y, core), inner: 32 (over x, z).
Axes of the slice: x: 4, y: 4, z: 8, core: 2. Of those that a mesh axis runs over, the one named last changes fastest.
Arguments:
- density: float32 [128, 64, 16384], P('inner', None, 'sector'), may hold values from -6 to 6
- source_sector: int32 [32, 8, 16], P('inner'), may hold values from 0 to 7, as said below
- source_tile: int32 [32, 8, 16], P('inner'), may hold values from 0 to 15
- matrix_id: int32 [32, 8, 16], P('inner'), may hold values from 0 to 31
- cubic_weights: float32 [32, 128, 128], replicated, may hold values from -0.6 to 1.5, as said below
- bin_cells: int32 [8, 32], P('sector'), may hold values from 1 to 128, 2048 in all within a row
- wave_level: float32 [8, 32], P('sector'), may hold values from 0.15 to 1
- energy_rate: float32 [128, 64], replicated, may hold values from 0.01 to 0.12
- pitch_rate: float32 [128, 64], replicated, may hold values from 0.01 to 0.12
Outputs:
- advanced: float32 [128, 64, 16384], P('inner', None, 'sector')
The draws below stay inside these ranges and needn't reach their ends.
Inputs may be any that keep to these rules, and one draw needn't show every extreme that they name: `source_sector`: for every energy block and destination sector, at most 3 of its 16 tiles depart from any one sector, exactly 3 depart from one sector, and that sector lies one to three sectors below the destination, cyclically. `cubic_weights`: every row of every matrix sums to one.
All inputs are finite; a program needn't handle non-finite values.
Results may differ from the reference program's by a relative error of at most 0.000096.
Values sent between devices are 32-bit elements; how exact they have to be, the bound alone decides.
A program may use at most 128 MiB of HBM per device.

```python
import math
import jax
import jax.numpy as jnp
import numpy as np
from jax import lax

E = 128
P_SIZE = 64
TILE = 128
NW = 32
PASSES = 12
NT = 16
EB = 4
CAP = 3
MAXC = 128
CELLS = 16384
N_SECTOR = 8
N_INNER = 32


def draw_source_sector(key, part):
    key_back, key_score, key_order = jax.random.split(jax.random.fold_in(key, 7), 3)
    rows = N_INNER * N_SECTOR
    dest = jnp.tile(jnp.arange(N_SECTOR, dtype=jnp.int32), N_INNER)
    back = jax.random.randint(key_back, (rows,), 0, 3)
    favoured = (dest - 1 - back) % N_SECTOR
    slot_sector = jnp.arange(N_SECTOR * CAP, dtype=jnp.int32) // CAP
    scores = jax.random.randint(key_score, (rows, N_SECTOR * CAP), 0, 1 << 20)
    scores = scores + jnp.where(slot_sector[None, :] == favoured[:, None], 1 << 21, 0)
    order = jnp.argsort(-scores, axis=1, stable=True)[:, :NT]
    chosen = slot_sector[order]
    shuffle = jax.random.randint(key_order, (rows, NT), 0, 1 << 20) * NT + jnp.arange(NT, dtype=jnp.int32)[None, :]
    mixed = jnp.take_along_axis(chosen, jnp.argsort(shuffle, axis=1), axis=1)
    return mixed.reshape(N_INNER, N_SECTOR, NT).astype(jnp.int32)


def draw_cubic_weights(key, part):
    frac = jax.random.uniform(jax.random.fold_in(key, 11), (NW, 1, 1), minval=0.15, maxval=0.85, dtype=jnp.float32)
    rows = jnp.arange(TILE, dtype=jnp.int32)[None, :, None]
    cols = jnp.arange(TILE, dtype=jnp.int32)[None, None, :]
    coeffs = [-frac * (frac - 1.0) * (frac - 2.0) / 6.0, (frac + 1.0) * (frac - 1.0) * (frac - 2.0) / 2.0, -(frac + 1.0) * frac * (frac - 2.0) / 2.0, (frac + 1.0) * frac * (frac - 1.0) / 6.0]
    total = jnp.zeros((NW, TILE, TILE), jnp.float32)
    for place in range(4):
        target = jnp.clip(rows + place - 1, 0, TILE - 1)
        total = total + coeffs[place] * (cols == target).astype(jnp.float32)
    spread = 0.3 * TILE ** (-0.5)
    noise_key = jax.random.fold_in(key, 13)
    noise = jnp.clip(jax.random.normal(noise_key, (NW, TILE, TILE), dtype=jnp.float32) * spread, -3.0 * spread, 3.0 * spread)
    noise = noise - jnp.mean(noise, axis=2, keepdims=True)
    return total + noise


def plant(array, key, smallest, top_value):
    longest = array.shape.index(max(array.shape))
    spots = []
    for shift in (0, 1):
        where = [jax.random.randint(jax.random.fold_in(key, axis), (), 0, length) for axis, length in enumerate(array.shape)]
        where[longest] = (where[longest] + shift) % array.shape[longest]
        spots.append(tuple(where))
    return array.at[spots[0]].set(smallest).at[spots[1]].set(top_value)


def block_scale(key, shape, pieces, low, largest):
    factor_of = 1.0
    for axis_at, blocks in pieces:
        heights = jax.random.uniform(jax.random.fold_in(jax.random.fold_in(key, 6), axis_at), (blocks,), jnp.float32, low / len(pieces), largest / len(pieces))
        factor_of = factor_of * jnp.repeat(jnp.exp(heights), shape[axis_at] // blocks).reshape((-1,) + (1,) * (len(shape) - 1 - axis_at))
    return factor_of


def split_up(number_of, total, most, slope):
    loads = [(1 << 20) // math.isqrt(grade ** slope) + 1 for grade in range(2, number_of + 1)]
    spare, counts = total - most - (number_of - 1), [1] * (number_of - 1)
    while spare > 0:
        free = [i for i in range(number_of - 1) if counts[i] < most]
        whole, remaining = sum([loads[i] for i in free]), spare
        for i in free:
            more = min(most - counts[i], max(1, remaining * loads[i] // whole), spare)
            counts[i] = counts[i] + more
            spare = spare - more
    return np.array([most] + counts)


def uneven_parts(stream_key, amount, total, bound, skew):
    if amount == 2:
        one = jax.random.randint(stream_key, (), max(1, total - bound), min(bound, total - 1) + 1)
        return jnp.stack([one, total - one])
    lengths = jnp.asarray(split_up(amount, total, bound, skew), jnp.int32)
    twos = (amount - 1) // 2
    giver, taker = lengths[1:1 + 2 * twos:2], lengths[2:2 + 2 * twos:2]
    room = jnp.minimum(giver - 1, bound - taker)
    shifted = jax.random.randint(jax.random.fold_in(stream_key, 1), (twos,), 0, 1 << 20) % (room + 1)
    lengths = lengths.at[1:1 + 2 * twos:2].set(giver - shifted).at[2:2 + 2 * twos:2].set(taker + shifted)
    return lengths[jax.random.permutation(jax.random.fold_in(stream_key, 2), amount)]


def normal_values(rng, shape, width, limit, shards=(), kind=jnp.bfloat16):
    drawn = width * jax.random.normal(rng, shape, jnp.float32)
    if shards:
        drawn = drawn * block_scale(rng, shape, shards, -0.22, 0.18)
    return jnp.clip(drawn, -limit, limit).astype(kind)


def setup_inputs(seed: int = 0) -> dict:
    seeds = jax.random.split(jax.random.key(seed), 10)
    return {
        "density": normal_values(seeds[0], (E, P_SIZE, CELLS), 1.0, 6.0, ((0, 32), (2, 8)), jnp.float32),
        "source_sector": draw_source_sector(jax.random.fold_in(seeds[9], 71), 0),
        "source_tile": plant(jax.random.randint(seeds[2], (N_INNER, N_SECTOR, NT), 0, NT), jax.random.fold_in(seeds[2], 1), 0, NT - 1).astype(jnp.int32),
        "matrix_id": plant(jax.random.randint(seeds[3], (N_INNER, N_SECTOR, NT), 0, NW), jax.random.fold_in(seeds[3], 1), 0, NW - 1).astype(jnp.int32),
        "cubic_weights": draw_cubic_weights(jax.random.fold_in(seeds[9], 71), 0),
        "bin_cells": jax.vmap(lambda own: uneven_parts(own, N_INNER, NT * TILE, MAXC, 2))(jax.random.split(seeds[5], N_SECTOR)).reshape((N_SECTOR, N_INNER)).astype(jnp.int32),
        "wave_level": jnp.clip(jnp.exp(math.log(1.0) - 1.89712 * jax.random.uniform(seeds[6], (N_SECTOR, N_INNER), jnp.float32) ** block_scale(seeds[6], (N_SECTOR, N_INNER), ((0, 8),), -0.2, 0.2)), 0.15, 1.0),
        "energy_rate": jnp.clip(jnp.exp(jax.random.uniform(seeds[7], (E, P_SIZE), jnp.float32, math.log(0.01), math.log(0.12))), 0.01, 0.12),
        "pitch_rate": jnp.clip(jnp.exp(jax.random.uniform(seeds[8], (E, P_SIZE), jnp.float32, math.log(0.01), math.log(0.12))), 0.01, 0.12),
    }


def drift_step(density, source_sector, source_tile, matrix_id, cubic_weights):
    shaped = density.reshape(N_INNER, EB, P_SIZE, N_SECTOR, NT, TILE)

    def one_block(block):
        local = shaped[block]
        sources = source_sector[block]
        departing = local[:, :, sources, source_tile[block], :]
        matrices = cubic_weights[matrix_id[block]]
        return jnp.einsum("epstj,stij->epsti", departing, matrices, precision=lax.Precision.HIGHEST)

    moved = lax.map(one_block, jnp.arange(N_INNER, dtype=jnp.int32))
    return moved.reshape(E, P_SIZE, CELLS)


def one_pass(field, rate_cell, energy_rate, pitch_rate):
    flux_e = energy_rate[:-1, :, None] * (field[1:] - field[:-1])
    flux_p = pitch_rate[:, :-1, None] * (field[:, 1:] - field[:, :-1])
    change_e = jnp.pad(flux_e, ((0, 1), (0, 0), (0, 0))) - jnp.pad(flux_e, ((1, 0), (0, 0), (0, 0)))
    change_p = jnp.pad(flux_p, ((0, 0), (0, 1), (0, 0))) - jnp.pad(flux_p, ((0, 0), (1, 0), (0, 0)))
    return field + rate_cell[None, None, :] * (change_e + change_p)


def reference(density, source_sector, source_tile, matrix_id, cubic_weights, bin_cells, wave_level, energy_rate, pitch_rate):
    cell_total = NT * TILE
    bin_ends = jnp.cumsum(bin_cells, axis=1)
    positions = jnp.arange(cell_total, dtype=jnp.int32)
    bin_of = jnp.sum((bin_ends[:, None, :] <= positions[None, :, None]).astype(jnp.int32), axis=2).astype(jnp.int32)
    levels = jnp.take_along_axis(wave_level, bin_of, axis=1)
    first = drift_step(density, source_sector, source_tile, matrix_id, cubic_weights)
    per_sector = jnp.moveaxis(first.reshape(E, P_SIZE, N_SECTOR, cell_total), 2, 0)

    def diffuse_sector(inputs):
        field, rate_cell = inputs

        def loop_body(step, current):
            return one_pass(current, rate_cell, energy_rate, pitch_rate)

        return lax.fori_loop(0, PASSES, loop_body, field)

    diffused = lax.map(diffuse_sector, (per_sector, levels))
    diffused = jnp.moveaxis(diffused, 0, 2).reshape(E, P_SIZE, CELLS)
    return drift_step(diffused, source_sector, source_tile, matrix_id, cubic_weights)
```

```python
import functools

import jax
import jax.numpy as jnp
from jax import lax
from jax.experimental import pallas as pl
from jax.experimental.pallas import tpu as pltpu
from jax.sharding import PartitionSpec as P

PASSES = 12
MESH = pl.DeviceIdType.MESH
F32 = jnp.float32
BF16 = jnp.bfloat16


def split(value):
    high = value.astype(BF16)
    low = (value - high.astype(F32)).astype(BF16)
    return high, low


def swap_halves(upper, lower, first_half):
    upper_rolled = pltpu.roll(upper, 64, 2)
    lower_rolled = pltpu.roll(lower, 64, 2)
    return (
        jnp.where(first_half, upper, lower_rolled),
        jnp.where(first_half, upper_rolled, lower),
    )


def kernel(
    src_ref,
    tile_ref,
    mid_ref,
    bins_ref,
    wave_ref,
    dens_ref,
    weight_ref,
    er_ref,
    pr_ref,
    out_ref,
    pick_ref,
    slot_ref,
    natural,
    tiles,
    send1,
    recv1_0,
    recv1_1,
    recv1_2,
    recv1_3,
    gath,
    field,
    other,
    back_0,
    back_1,
    back_2,
    back_3,
    send2,
    recv2_0,
    recv2_1,
    recv2_2,
    recv2_3,
    coef_e,
    coef_p,
    wprep,
    s_a,
    r_a,
    s_c,
    r_c,
    s_e,
    r_e,
    s_f,
    r_f,
):
    recv1 = (recv1_0, recv1_1, recv1_2, recv1_3)
    back = (back_0, back_1, back_2, back_3)
    recv2 = (recv2_0, recv2_1, recv2_2, recv2_3)
    s = lax.axis_index("sector")
    i = lax.axis_index("inner")

    def sector_at(m):
        return lax.rem(s + 3 * (m + 1), 8)

    barrier = pltpu.get_barrier_semaphore()
    for m in range(7):
        pl.semaphore_signal(barrier, inc=1, device_id=(sector_at(m), i), device_id_type=MESH)
    for off in range(1, 32):
        pl.semaphore_signal(
            barrier, inc=1, device_id=(s, lax.rem(i + off, 32)), device_id_type=MESH
        )

    for d in range(8):
        count = jnp.int32(0)
        picks = [jnp.int32(0)] * 3
        for t in range(16):
            hit = src_ref[d, t] == s
            tile = tile_ref[d, t]
            for r in range(3):
                picks[r] = jnp.where(hit & (count == r), tile, picks[r])
            count = count + hit.astype(jnp.int32)
        for r in range(3):
            pick_ref[d * 3 + r] = picks[r]

    for e in range(4):
        for t in range(16):
            natural[t] = dens_ref[e, :, t * 128 : (t + 1) * 128]
        for t in range(16):
            for half in range(2):
                for q in range(4):
                    to = half * 32 + q * 8
                    tiles[e, t, to : to + 8, :] = natural[
                        t, pl.ds(half * 32 + q, 8, stride=4), :
                    ]
        for m in range(7):
            for r in range(3):
                send1[e, m, r] = tiles[e, pick_ref[sector_at(m) * 3 + r]]
        for r in range(3):
            recv1[e][s * 3 + r] = tiles[e, pick_ref[s * 3 + r]]

    pl.semaphore_wait(barrier, 38)

    for e in range(4):

        def send_first(m, _, e=e):
            pltpu.make_async_remote_copy(
                send1.at[e, m],
                recv1[e].at[pl.ds(s * 3, 3)],
                s_a.at[e],
                r_a.at[e],
                device_id=(sector_at(m), i),
                device_id_type=MESH,
            ).start()
            return 0

        lax.fori_loop(0, 7, send_first, 0)

    own = [src_ref[s, t] for t in range(16)]
    for t in range(16):
        rank = jnp.int32(0)
        for u in range(t):
            rank = rank + (own[u] == own[t]).astype(jnp.int32)
        slot_ref[t] = own[t] * 3 + rank

    for t in range(16):
        high, low = split(weight_ref[mid_ref[s, t]].T)
        wprep[t, 0:128, 0:128] = high
        wprep[t, 128:256, 0:128] = high
        wprep[t, 0:128, 128:256] = low
        wprep[t, 128:256, 128:256] = low

    lanes = lax.broadcasted_iota(jnp.int32, (4, 8, 128), 2)
    first_half = lanes < 64

    def interpolate(rows, t):
        high, low = split(rows)
        both = jnp.dot(
            jnp.concatenate([high, low], axis=1), wprep[t], preferred_element_type=F32
        )
        return both[:, 0:128] + both[:, 128:256]

    def first_drift(e):
        pltpu.make_async_copy(
            recv1[e].at[pl.ds(0, 21)], recv1[e].at[pl.ds(0, 21)], r_a.at[e]
        ).wait()

        def halves(t):
            moved = interpolate(recv1[e][slot_ref[t]], t)
            return swap_halves(
                moved[0:32].reshape(4, 8, 128), moved[32:64].reshape(4, 8, 128), first_half
            )

        def send(place, target):
            pltpu.make_async_remote_copy(
                gath.at[e, place],
                field.at[i * 4 + e],
                s_c.at[e],
                r_c,
                device_id=(s, target),
                device_id_type=MESH,
            ).start()

        for step in range(15):
            t = lax.rem(i // 2 + 3 * (step + 1), 16)
            outs = halves(t)
            for half in range(2):
                gath[e, step * 2 + half] = outs[half]
                send(step * 2 + half, t * 2 + half)
        outs = halves(i // 2)
        odd = lax.rem(i, 2) == 1
        field[i * 4 + e] = jnp.where(odd, outs[1], outs[0])
        gath[e, 30] = jnp.where(odd, outs[0], outs[1])
        send(30, i + 1 - 2 * lax.rem(i, 2))

    for e in range(4):
        first_drift(e)

    lane_row = lax.broadcasted_iota(jnp.int32, (1, 128), 1)
    cell = i * 64 + lax.rem(lane_row, 64)
    level = jnp.zeros((1, 128), F32)
    start = jnp.int32(0)
    for k in range(32):
        level = jnp.where(cell >= start, wave_ref[0, k], level)
        start = start + bins_ref[0, k]
    row = lax.broadcasted_iota(jnp.int32, (32, 64), 0)
    pitch = lax.broadcasted_iota(jnp.int32, (32, 64), 1)
    chosen = lax.rem(pitch, 32) == lax.rem(row, 8) * 4 + row // 8
    mask_e = chosen.astype(F32)
    mask_p = (chosen & (pitch < 63)).astype(F32)
    half_of = (
        lax.broadcasted_iota(jnp.int32, (64, 128), 0) // 32
        == lax.broadcasted_iota(jnp.int32, (64, 128), 1) // 64
    ).astype(F32)
    sub = lax.broadcasted_iota(jnp.int32, (8, 64), 0)

    def spread(rates, mask):
        wide = (rates[:, None, :] * mask[None]).reshape(256, 64)
        full = jnp.dot(
            wide, half_of, precision=lax.Precision.HIGHEST, preferred_element_type=F32
        )
        return (full * level).reshape(8, 4, 8, 128)

    def coefficients(b, _):
        at = pl.ds(pl.multiple_of(b * 8, 8), 8)
        rates = jnp.where(b * 8 + sub < 127, er_ref[at, :], 0.0)
        coef_e[at] = spread(rates, mask_e)
        coef_p[at] = spread(pr_ref[at, :], mask_p)
        return 0

    lax.fori_loop(0, 16, coefficients, 0)
    field[128] = jnp.zeros((4, 8, 128), F32)
    other[128] = jnp.zeros((4, 8, 128), F32)

    pltpu.make_async_copy(field.at[pl.ds(0, 124)], field.at[pl.ds(0, 124)], r_c).wait()

    sublane = lax.broadcasted_iota(jnp.int32, (8, 128), 0)
    top, bottom = sublane == 0, sublane == 7

    def one_pass(source, target):
        def rows(b, carry):
            now, flux_before = carry
            for k in range(8):
                e = b * 8 + k
                later = source[e + 1]
                flux = coef_e[e] * (later - now)
                shifted = pltpu.roll(now[0], 7, 0)
                shifted = jnp.where(bottom, pltpu.roll(shifted, 64, 1), shifted)
                pitch_flux = [
                    coef_p[e, q] * ((now[q + 1] if q < 3 else shifted) - now[q])
                    for q in range(4)
                ]
                wrapped = pltpu.roll(pitch_flux[3], 1, 0)
                wrapped = jnp.where(top, pltpu.roll(wrapped, 64, 1), wrapped)
                for q in range(4):
                    below = pitch_flux[q - 1] if q else wrapped
                    target[e, q] = now[q] + (
                        (flux[q] - flux_before[q]) + (pitch_flux[q] - below)
                    )
                now, flux_before = later, flux
            return now, flux_before

        lax.fori_loop(0, 16, rows, (source[0], jnp.zeros((4, 8, 128), F32)))

    def two_passes(_, carry):
        one_pass(field, other)
        one_pass(other, field)
        return carry

    lax.fori_loop(0, PASSES // 2, two_passes, 0)

    for e in range(4):

        def send_back(n, _, e=e):
            target = lax.rem(i + 13 * (n + 1), 32)
            pltpu.make_async_remote_copy(
                field.at[target * 4 + e],
                back[e].at[i],
                s_e.at[e],
                r_e.at[e],
                device_id=(s, target),
                device_id_type=MESH,
            ).start()
            return 0

        lax.fori_loop(0, 31, send_back, 0)
        back[e][i] = field[i * 4 + e]

    def pack_second(e):
        pltpu.make_async_copy(
            back[e].at[pl.ds(0, 31)], back[e].at[pl.ds(0, 31)], r_e.at[e]
        ).wait()

        def pack(d, ref, lead, place):
            for r in range(3):
                tile = pick_ref[d * 3 + r]
                outs = swap_halves(back[e][tile * 2], back[e][tile * 2 + 1], first_half)
                for half in range(2):
                    for q in range(4):
                        at = pl.ds(half * 32 + q, 8, stride=4)
                        ref[(*lead, place + r, at, slice(None))] = outs[half][q]

        for m in range(7):
            d = sector_at(m)
            pack(d, send2, (e, m), 0)
            pltpu.make_async_remote_copy(
                send2.at[e, m],
                recv2[e].at[pl.ds(s * 3, 3)],
                s_f.at[e],
                r_f.at[e],
                device_id=(d, i),
                device_id_type=MESH,
            ).start()
        pack(s, recv2[e], (), s * 3)

    def second_drift(e):
        pltpu.make_async_copy(
            recv2[e].at[pl.ds(0, 21)], recv2[e].at[pl.ds(0, 21)], r_f.at[e]
        ).wait()

        for t in range(16):
            out_ref[e, :, t * 128 : (t + 1) * 128] = interpolate(recv2[e][slot_ref[t]], t)

    pack_second(0)
    for e in range(1, 4):
        pack_second(e)
        second_drift(e - 1)
    second_drift(3)

    def drain(e, _):
        pltpu.make_async_copy(send1.at[e, pl.ds(0, 7)], send1.at[e, pl.ds(0, 7)], s_a.at[e]).wait()
        pltpu.make_async_copy(gath.at[e, pl.ds(0, 31)], gath.at[e, pl.ds(0, 31)], s_c.at[e]).wait()
        pltpu.make_async_copy(field.at[pl.ds(0, 31)], field.at[pl.ds(0, 31)], s_e.at[e]).wait()
        pltpu.make_async_copy(send2.at[e, pl.ds(0, 7)], send2.at[e, pl.ds(0, 7)], s_f.at[e]).wait()
        return 0

    lax.fori_loop(0, 4, drain, 0)


def shards(
    density,
    source_sector,
    source_tile,
    matrix_id,
    cubic_weights,
    bin_cells,
    wave_level,
    energy_rate,
    pitch_rate,
):
    vmem = pl.BlockSpec(memory_space=pltpu.VMEM)
    smem = pl.BlockSpec(memory_space=pltpu.SMEM)
    dma = pltpu.SemaphoreType.DMA
    return pl.pallas_call(
        kernel,
        out_shape=jax.ShapeDtypeStruct((4, 64, 2048), F32),
        in_specs=[smem] * 5 + [vmem] * 4,
        out_specs=vmem,
        scratch_shapes=[
            pltpu.SMEM((24,), jnp.int32),
            pltpu.SMEM((16,), jnp.int32),
            pltpu.VMEM((16, 64, 128), F32),
            pltpu.VMEM((4, 16, 64, 128), F32),
            pltpu.VMEM((4, 7, 3, 64, 128), F32),
            *[pltpu.VMEM((24, 64, 128), F32)] * 4,
            pltpu.VMEM((4, 31, 4, 8, 128), F32),
            pltpu.VMEM((129, 4, 8, 128), F32),
            pltpu.VMEM((129, 4, 8, 128), F32),
            *[pltpu.VMEM((32, 4, 8, 128), F32)] * 4,
            pltpu.VMEM((4, 7, 3, 64, 128), F32),
            *[pltpu.VMEM((24, 64, 128), F32)] * 4,
            pltpu.VMEM((128, 4, 8, 128), F32),
            pltpu.VMEM((128, 4, 8, 128), F32),
            pltpu.VMEM((16, 256, 256), BF16),
            dma((4,)),
            dma((4,)),
            dma((4,)),
            dma,
            dma((4,)),
            dma((4,)),
            dma((4,)),
            dma((4,)),
        ],
        compiler_params=pltpu.CompilerParams(
            collective_id=0, has_side_effects=True, vmem_limit_bytes=50 * 2**20
        ),
        name="ion_step",
    )(
        source_sector[0],
        source_tile[0],
        matrix_id[0],
        bin_cells,
        wave_level,
        density,
        cubic_weights,
        energy_rate,
        pitch_rate,
    )


def solution(mesh):
    return jax.shard_map(
        shards,
        mesh=mesh,
        in_specs=(
            P("inner", None, "sector"),
            P("inner", None, None),
            P("inner", None, None),
            P("inner", None, None),
            P(),
            P("sector", None),
            P("sector", None),
            P(),
            P(),
        ),
        out_specs=P("inner", None, "sector"),
        check_vma=False,
    )
```

```python
import jax
import jax.numpy as jnp
from jax import lax
from jax.experimental import pallas as pl
from jax.experimental.pallas import tpu as pltpu
from jax.sharding import PartitionSpec as P

PASSES = 12
MESH = pl.DeviceIdType.MESH
F32 = jnp.float32
BF16 = jnp.bfloat16


def split(value):
    high = value.astype(BF16)
    low = (value - high.astype(F32)).astype(BF16)
    return high, low


def turn(blocks, far, near):
    b0, b1, b2, b3 = blocks

    def exchange(low, high, first, width):
        return (
            jnp.where(first, low, pltpu.roll(high, width, 2)),
            jnp.where(first, pltpu.roll(low, 128 - width, 2), high),
        )

    b0, b2 = exchange(b0, b2, far, 64)
    b1, b3 = exchange(b1, b3, far, 64)
    b0, b1 = exchange(b0, b1, near, 32)
    b2, b3 = exchange(b2, b3, near, 32)
    return b0, b1, b2, b3


def kernel(*refs):
    refs = list(refs)

    def take(count):
        out = refs[:count]
        del refs[:count]
        return out

    (src_in, tile_in, mid_in, bins_in, wave_in, dens_in, weight_in, er_in, pr_in) = take(9)
    (out_ref,) = take(1)
    src_ref, tile_ref, mid_ref, bins_ref, wave_ref, pick_ref, slot_ref = take(7)
    natural = take(4)
    tiles, weight_ref, er_ref, pr_ref, er_rows, pr_rows, send1 = take(7)
    recv1 = take(4)
    (gath,) = take(1)
    field = take(2)
    (other,) = take(1)
    coef_e = take(2)
    coef_p = take(2)
    back = [take(4) for _ in range(2)]
    (send2,) = take(1)
    recv2 = [take(4) for _ in range(2)]
    wprep, order_buf = take(2)
    t_sem, d_sem, w_sem, s_a, r_a, s_c, r_c, s_e, r_e, s_f, r_f = take(11)

    s = lax.axis_index("sector")
    i = lax.axis_index("inner")

    def sector_at(m):
        return lax.rem(s + 3 * (m + 1), 8)

    barrier = pltpu.get_barrier_semaphore()
    for m in range(7):
        pl.semaphore_signal(barrier, inc=1, device_id=(sector_at(m), i), device_id_type=MESH)
    for off in range(1, 32):
        pl.semaphore_signal(
            barrier, inc=1, device_id=(s, lax.rem(i + off, 32)), device_id_type=MESH
        )

    tables = [
        pltpu.make_async_copy(a, b, t_sem.at[n])
        for n, (a, b) in enumerate(
            (
                (src_in, src_ref),
                (tile_in, tile_ref),
                (mid_in, mid_ref),
                (bins_in, bins_ref),
                (wave_in, wave_ref),
            )
        )
    ]
    for copy in tables:
        copy.start()
    for e in range(4):
        for t in range(16):
            pltpu.make_async_copy(
                dens_in.at[e, :, t * 128 : (t + 1) * 128], natural[e].at[t], d_sem.at[e]
            ).start()
    parameters = [
        pltpu.make_async_copy(a, b, w_sem.at[n])
        for n, (a, b) in enumerate(
            ((weight_in, weight_ref), (er_in, er_ref), (pr_in, pr_ref))
        )
    ]
    for copy in parameters:
        copy.start()
    for copy in tables:
        copy.wait()

    for d in range(8):
        count = jnp.int32(0)
        picks = [jnp.int32(0)] * 3
        for t in range(16):
            hit = src_ref[0, d, t] == s
            tile = tile_ref[0, d, t]
            for r in range(3):
                picks[r] = jnp.where(hit & (count == r), tile, picks[r])
            count = count + hit.astype(jnp.int32)
        for r in range(3):
            pick_ref[d * 3 + r] = picks[r]

    def pack_first(e):
        pltpu.make_async_copy(natural[e], natural[e], d_sem.at[e]).wait()
        for t in range(16):
            for quarter in range(4):
                for q in range(2):
                    to = quarter * 16 + q * 8
                    tiles[e, t, to : to + 8, :] = natural[e][
                        t, pl.ds(quarter * 16 + q, 8, stride=2), :
                    ]
        for m in range(7):
            for r in range(3):
                send1[e, m, r] = tiles[e, pick_ref[sector_at(m) * 3 + r]]
        for r in range(3):
            recv1[e][s * 3 + r] = tiles[e, pick_ref[s * 3 + r]]

    def send_first(e):
        def one(m, _):
            pltpu.make_async_remote_copy(
                send1.at[e, m],
                recv1[e].at[pl.ds(s * 3, 3)],
                s_a.at[e],
                r_a.at[e],
                device_id=(sector_at(m), i),
                device_id_type=MESH,
            ).start()
            return 0

        lax.fori_loop(0, 7, one, 0)

    pack_first(0)
    pl.semaphore_wait(barrier, 38)
    send_first(0)
    for e in range(1, 4):
        pack_first(e)
        send_first(e)

    own = [src_ref[0, s, t] for t in range(16)]
    for t in range(16):
        rank = jnp.int32(0)
        for u in range(t):
            rank = rank + (own[u] == own[t]).astype(jnp.int32)
        slot_ref[t] = own[t] * 3 + rank

    for copy in parameters:
        copy.wait()
    for t in range(16):
        high, low = split(weight_ref[mid_ref[0, s, t]].T)
        wprep[t, 0:128, 0:128] = high
        wprep[t, 128:256, 0:128] = high
        wprep[t, 0:128, 128:256] = low
        wprep[t, 128:256, 128:256] = low

    er_rows[...] = er_ref[...].T
    pr_rows[...] = pr_ref[...].T
    lane_row = lax.broadcasted_iota(jnp.int32, (1, 128), 1)
    levels = []
    for a in range(2):
        cell = i * 64 + a * 32 + lax.rem(lane_row, 32)
        level = jnp.zeros((1, 128), F32)
        start = jnp.int32(0)
        for k in range(32):
            level = jnp.where(cell >= start, wave_ref[0, k], level)
            start = start + bins_ref[0, k]
        levels.append(level)
    row = lax.broadcasted_iota(jnp.int32, (16, 64), 0)
    pitch = lax.broadcasted_iota(jnp.int32, (16, 64), 1)
    chosen = lax.rem(pitch, 16) == lax.rem(row, 8) * 2 + row // 8
    mask_e = chosen.astype(F32)
    mask_p = (chosen & (pitch < 63)).astype(F32)
    quarter_of = (
        lax.broadcasted_iota(jnp.int32, (64, 128), 0) // 16
        == lax.broadcasted_iota(jnp.int32, (64, 128), 1) // 32
    ).astype(F32)
    sub = lax.broadcasted_iota(jnp.int32, (8, 64), 0)

    def spread(rates, mask):
        wide = (rates[:, None, :] * mask[None]).reshape(128, 64)
        return jnp.dot(
            wide, quarter_of, precision=lax.Precision.HIGHEST, preferred_element_type=F32
        )

    def coefficients(b, _):
        at = pl.ds(pl.multiple_of(b * 8, 8), 8)
        along_e = spread(jnp.where(b * 8 + sub < 127, er_rows[at, :], 0.0), mask_e)
        along_p = spread(pr_rows[at, :], mask_p)
        for a in range(2):
            coef_e[a][at] = (along_e * levels[a]).reshape(8, 2, 8, 128)
            coef_p[a][at] = (along_p * levels[a]).reshape(8, 2, 8, 128)
        return 0

    lax.fori_loop(0, 16, coefficients, 0)
    zero_row = jnp.zeros((2, 8, 128), F32)
    field[0][128] = zero_row
    field[1][128] = zero_row
    other[128] = zero_row

    lanes = lax.broadcasted_iota(jnp.int32, (2, 8, 128), 2)
    far = lanes < 64
    near = lax.rem(lanes, 64) < 32

    def interpolate(rows, t):
        high, low = split(rows)
        both = jnp.dot(
            jnp.concatenate([high, low], axis=1), wprep[t], preferred_element_type=F32
        )
        return both[:, 0:128] + both[:, 128:256]

    def send_on(e, a, place, target):
        pltpu.make_async_remote_copy(
            gath.at[a, e, place],
            field[a].at[i * 4 + e],
            s_c.at[a],
            r_c.at[a],
            device_id=(s, target),
            device_id_type=MESH,
        ).start()

    partner = i + 1 - 2 * lax.rem(i, 2)

    def first_drift(e):
        pltpu.make_async_copy(
            recv1[e].at[pl.ds(0, 21)], recv1[e].at[pl.ds(0, 21)], r_a.at[e]
        ).wait()
        for step in range(16):
            t = lax.rem(i // 2 + 3 * (step + 1), 16)
            moved = interpolate(recv1[e][slot_ref[t]], t).reshape(4, 2, 8, 128)
            outs = turn([moved[q] for q in range(4)], far, near)
            if step < 15:
                for half in range(2):
                    for a in range(2):
                        gath[a, e, step * 2 + half] = outs[half * 2 + a]
                    send_on(e, 0, step * 2 + half, t * 2 + half)
            else:
                odd = lax.rem(i, 2) == 1
                for a in range(2):
                    field[a][i * 4 + e] = jnp.where(odd, outs[2 + a], outs[a])
                    gath[a, e, 30] = jnp.where(odd, outs[a], outs[2 + a])
                send_on(e, 0, 30, partner)

    def send_rest(e):
        def one(step, _):
            t = lax.rem(i // 2 + 3 * (step + 1), 16)
            for half in range(2):
                send_on(e, 1, step * 2 + half, t * 2 + half)
            return 0

        lax.fori_loop(0, 15, one, 0)
        send_on(e, 1, 30, partner)

    first_drift(0)
    send_rest(0)
    first_drift(1)
    first_drift(2)
    send_rest(1)
    first_drift(3)
    send_rest(2)
    send_rest(3)

    sublane = lax.broadcasted_iota(jnp.int32, (8, 128), 0)
    top, bottom = sublane == 0, sublane == 7

    def one_pass(source, target, along_e, along_p):
        def rows(b, carry):
            now, flux_before = carry
            for k in range(32):
                e = b * 32 + k
                later = source[e + 1]
                flux = along_e[e] * (later - now)
                shifted = pltpu.roll(now[0], 7, 0)
                shifted = jnp.where(bottom, pltpu.roll(shifted, 96, 1), shifted)
                pitch_low = along_p[e, 0] * (now[1] - now[0])
                pitch_high = along_p[e, 1] * (shifted - now[1])
                wrapped = pltpu.roll(pitch_high, 1, 0)
                wrapped = jnp.where(top, pltpu.roll(wrapped, 32, 1), wrapped)
                target[e, 0] = now[0] + ((flux[0] - flux_before[0]) + (pitch_low - wrapped))
                target[e, 1] = now[1] + ((flux[1] - flux_before[1]) + (pitch_high - pitch_low))
                now, flux_before = later, flux
            return now, flux_before

        lax.fori_loop(0, 4, rows, (source[0], zero_row))

    def diffuse(a):
        pltpu.make_async_copy(
            field[a].at[pl.ds(0, 124)], field[a].at[pl.ds(0, 124)], r_c.at[a]
        ).wait()

        def two_passes(_, carry):
            one_pass(field[a], other, coef_e[a], coef_p[a])
            one_pass(other, field[a], coef_e[a], coef_p[a])
            return carry

        lax.fori_loop(0, PASSES // 2, two_passes, 0)

    def send_back(a):
        for e in range(4):

            def one(n, _, e=e):
                target = lax.rem(i + 13 * (n + 1), 32)
                pltpu.make_async_remote_copy(
                    field[a].at[target * 4 + e],
                    back[a][e].at[i],
                    s_e.at[a],
                    r_e.at[a, e],
                    device_id=(s, target),
                    device_id_type=MESH,
                ).start()
                return 0

            lax.fori_loop(0, 31, one, 0)
            back[a][e][i] = field[a][i * 4 + e]

    for a in range(2):
        diffuse(a)
        send_back(a)

    def pack_second(a, e):
        here = back[a][e]
        pltpu.make_async_copy(here.at[pl.ds(0, 31)], here.at[pl.ds(0, 31)], r_e.at[a, e]).wait()
        for m in range(8):
            d = sector_at(m)
            for r in range(3):
                tile = pick_ref[d * 3 + r]
                for half in range(2):
                    piece = here[tile * 2 + half]
                    if m < 7:
                        send2[a, e, m, r, half] = piece
                    else:
                        recv2[a][e][s * 3 + r, half] = piece
            if m < 7:
                pltpu.make_async_remote_copy(
                    send2.at[a, e, m],
                    recv2[a][e].at[pl.ds(s * 3, 3)],
                    s_f.at[a],
                    r_f.at[a, e],
                    device_id=(d, i),
                    device_id_type=MESH,
                ).start()

    def second_drift(e):
        for a in range(2):
            there = recv2[a][e]
            pltpu.make_async_copy(
                there.at[pl.ds(0, 21)], there.at[pl.ds(0, 21)], r_f.at[a, e]
            ).wait()
        for t in range(16):
            slot = slot_ref[t]
            pieces = [recv2[a][e][slot] for a in range(2)]
            outs = turn([pieces[a][half] for half in range(2) for a in range(2)], far, near)
            rows = jnp.concatenate([out.reshape(16, 128) for out in outs], axis=0)
            moved = interpolate(rows, t)
            for quarter in range(4):
                for q in range(2):
                    at = quarter * 16 + q * 8
                    order_buf[t, pl.ds(quarter * 16 + q, 8, stride=2), :] = moved[at : at + 8]
            out_ref[e, :, t * 128 : (t + 1) * 128] = order_buf[t]

    for e in range(4):
        pack_second(0, e)
    pack_second(1, 0)
    for e in range(1, 4):
        pack_second(1, e)
        second_drift(e - 1)
    second_drift(3)

    for e in range(4):
        pltpu.make_async_copy(
            send1.at[e, pl.ds(0, 7)], send1.at[e, pl.ds(0, 7)], s_a.at[e]
        ).wait()
    for a in range(2):
        for ref, sem in ((gath, s_c), (send2, s_f)):
            pltpu.make_async_copy(ref.at[a], ref.at[a], sem.at[a]).wait()
        pltpu.make_async_copy(
            field[a].at[pl.ds(0, 124)], field[a].at[pl.ds(0, 124)], s_e.at[a]
        ).wait()


def shards(
    density,
    source_sector,
    source_tile,
    matrix_id,
    cubic_weights,
    bin_cells,
    wave_level,
    energy_rate,
    pitch_rate,
):
    whole = pl.BlockSpec(memory_space=pltpu.VMEM)
    place = pl.BlockSpec(memory_space=pltpu.HBM)
    dma = pltpu.SemaphoreType.DMA

    def vmem(*shape):
        return pltpu.VMEM(shape, F32)

    return pl.pallas_call(
        kernel,
        out_shape=jax.ShapeDtypeStruct((4, 64, 2048), F32),
        in_specs=[place] * 9,
        out_specs=whole,
        scratch_shapes=[
            *[pltpu.SMEM((1, 8, 16), jnp.int32)] * 3,
            pltpu.SMEM((1, 32), jnp.int32),
            pltpu.SMEM((1, 32), F32),
            pltpu.SMEM((24,), jnp.int32),
            pltpu.SMEM((16,), jnp.int32),
            *[vmem(16, 64, 128)] * 4,
            vmem(4, 16, 64, 128),
            vmem(32, 128, 128),
            vmem(64, 128),
            vmem(64, 128),
            vmem(128, 64),
            vmem(128, 64),
            vmem(4, 7, 3, 64, 128),
            *[vmem(24, 64, 128)] * 4,
            vmem(2, 4, 31, 2, 8, 128),
            *[vmem(129, 2, 8, 128)] * 3,
            *[vmem(128, 2, 8, 128)] * 4,
            *[vmem(32, 2, 8, 128)] * 8,
            vmem(2, 4, 7, 3, 2, 2, 8, 128),
            *[vmem(24, 2, 2, 8, 128)] * 8,
            pltpu.VMEM((16, 256, 256), BF16),
            vmem(16, 64, 128),
            dma((5,)),
            dma((4,)),
            dma((3,)),
            dma((4,)),
            dma((4,)),
            dma((2,)),
            dma((2,)),
            dma((2,)),
            dma((2, 4)),
            dma((2,)),
            dma((2, 4)),
        ],
        compiler_params=pltpu.CompilerParams(
            collective_id=0, has_side_effects=True, vmem_limit_bytes=67043328
        ),
        name="ion_step",
    )(
        source_sector,
        source_tile,
        matrix_id,
        bin_cells,
        wave_level,
        density,
        cubic_weights,
        energy_rate.T,
        pitch_rate.T,
    )


def solution(mesh):
    return jax.shard_map(
        shards,
        mesh=mesh,
        in_specs=(
            P("inner", None, "sector"),
            P("inner", None, None),
            P("inner", None, None),
            P("inner", None, None),
            P(),
            P("sector", None),
            P("sector", None),
            P(),
            P(),
        ),
        out_specs=P("inner", None, "sector"),
        check_vma=False,
    )
```

```python
import jax
import jax.numpy as jnp
from jax import lax
from jax.experimental import pallas as pl
from jax.experimental.pallas import tpu as pltpu
from jax.sharding import PartitionSpec as P

PASSES = 12
MESH = pl.DeviceIdType.MESH
FIRST = ((0, 0, 1), (0, 1, 1), (1, 0, 2), (2, 0, 2), (3, 0, 2))
LAST = (
    ((0, 0, 2), (1, 0, 2), (2, 0, 2), (3, 0, 2)),
    ((0, 0, 2), (1, 0, 2), (2, 0, 2), (3, 0, 1), (3, 1, 1)),
)
F32 = jnp.float32
BF16 = jnp.bfloat16


def split(value):
    high = value.astype(BF16)
    low = (value - high.astype(F32)).astype(BF16)
    return high, low


def turn(blocks, far, near):
    b0, b1, b2, b3 = blocks

    def exchange(low, high, first, width):
        return (
            jnp.where(first, low, pltpu.roll(high, width, 2)),
            jnp.where(first, pltpu.roll(low, 128 - width, 2), high),
        )

    b0, b2 = exchange(b0, b2, far, 64)
    b1, b3 = exchange(b1, b3, far, 64)
    b0, b1 = exchange(b0, b1, near, 32)
    b2, b3 = exchange(b2, b3, near, 32)
    return b0, b1, b2, b3


def kernel(*refs):
    refs = list(refs)

    def take(count):
        out = refs[:count]
        del refs[:count]
        return out

    (src_in, tile_in, mid_in, bins_in, wave_in, dens_in, weight_in, er_in, pr_in) = take(9)
    (out_ref,) = take(1)
    src_ref, tile_ref, mid_ref, bins_ref, wave_ref, pick_ref, slot_ref = take(7)
    natural = take(4)
    tiles, weight_ref, er_ref, pr_ref, er_rows, pr_rows = take(6)
    send1 = take(5)
    recv1 = take(5)
    gath = [take(2) for _ in range(5)]
    field = take(2)
    (other,) = take(1)
    coef_e = take(2)
    coef_p = take(2)
    back = [take(len(LAST[a])) for a in range(2)]
    send2 = [take(len(LAST[a])) for a in range(2)]
    recv2 = [take(len(LAST[a])) for a in range(2)]
    wprep, order_buf = take(2)
    t_sem, d_sem, w_sem, s_a, r_a, s_c, r_c, s_e, r_e, s_f, r_f = take(11)

    s = lax.axis_index("sector")
    i = lax.axis_index("inner")

    def sector_at(m):
        return lax.rem(s + 3 * (m + 1), 8)

    barrier = pltpu.get_barrier_semaphore()
    for m in range(7):
        pl.semaphore_signal(barrier, inc=1, device_id=(sector_at(m), i), device_id_type=MESH)
    for off in range(1, 32):
        pl.semaphore_signal(
            barrier, inc=1, device_id=(s, lax.rem(i + off, 32)), device_id_type=MESH
        )

    tables = [
        pltpu.make_async_copy(a, b, t_sem.at[n])
        for n, (a, b) in enumerate(
            (
                (src_in, src_ref),
                (tile_in, tile_ref),
                (mid_in, mid_ref),
                (bins_in, bins_ref),
                (wave_in, wave_ref),
            )
        )
    ]
    for copy in tables:
        copy.start()
    for e in range(4):
        for t in range(16):
            pltpu.make_async_copy(
                dens_in.at[e, :, t * 128 : (t + 1) * 128], natural[e].at[t], d_sem.at[e]
            ).start()
    parameters = [
        pltpu.make_async_copy(a, b, w_sem.at[n])
        for n, (a, b) in enumerate(
            ((weight_in, weight_ref), (er_in, er_ref), (pr_in, pr_ref))
        )
    ]
    for copy in parameters:
        copy.start()
    for copy in tables:
        copy.wait()

    for d in range(8):
        count = jnp.int32(0)
        picks = [jnp.int32(0)] * 3
        for t in range(16):
            hit = src_ref[0, d, t] == s
            tile = tile_ref[0, d, t]
            for r in range(3):
                picks[r] = jnp.where(hit & (count == r), tile, picks[r])
            count = count + hit.astype(jnp.int32)
        for r in range(3):
            pick_ref[d * 3 + r] = picks[r]

    def pack_energy(e):
        pltpu.make_async_copy(natural[e], natural[e], d_sem.at[e]).wait()
        for t in range(16):
            for quarter in range(4):
                for q in range(2):
                    to = quarter * 8 + q * 32
                    tiles[e, t, to : to + 8, :] = natural[e][
                        t, pl.ds(quarter * 16 + q, 8, stride=2), :
                    ]

    def pack_first(c):
        e, q, n = FIRST[c]
        for m in range(8):
            for r in range(3):
                block = tiles[e, pick_ref[sector_at(m) * 3 + r], 32 * q : 32 * (q + n), :]
                if m < 7:
                    send1[c][m, r] = block
                else:
                    recv1[c][s * 3 + r] = block

    def send_first(c):
        def one(m, _):
            pltpu.make_async_remote_copy(
                send1[c].at[m],
                recv1[c].at[pl.ds(s * 3, 3)],
                s_a.at[c],
                r_a.at[c],
                device_id=(sector_at(m), i),
                device_id_type=MESH,
            ).start()
            return 0

        lax.fori_loop(0, 7, one, 0)

    pack_energy(0)
    pack_first(0)
    pl.semaphore_wait(barrier, 38)
    send_first(0)
    pack_first(1)
    send_first(1)
    for c in range(2, 5):
        pack_energy(FIRST[c][0])
        pack_first(c)
        send_first(c)

    own = [src_ref[0, s, t] for t in range(16)]
    for t in range(16):
        rank = jnp.int32(0)
        for u in range(t):
            rank = rank + (own[u] == own[t]).astype(jnp.int32)
        slot_ref[t] = own[t] * 3 + rank

    for copy in parameters:
        copy.wait()
    for t in range(16):
        high, low = split(weight_ref[mid_ref[0, s, t]].T)
        wprep[t, 0:128, 0:128] = high
        wprep[t, 128:256, 0:128] = high
        wprep[t, 0:128, 128:256] = low
        wprep[t, 128:256, 128:256] = low

    er_rows[...] = er_ref[...].T
    pr_rows[...] = pr_ref[...].T
    lane_row = lax.broadcasted_iota(jnp.int32, (1, 128), 1)
    levels = []
    for a in range(2):
        cell = i * 64 + a * 32 + lax.rem(lane_row, 32)
        level = jnp.zeros((1, 128), F32)
        start = jnp.int32(0)
        for k in range(32):
            level = jnp.where(cell >= start, wave_ref[0, k], level)
            start = start + bins_ref[0, k]
        levels.append(level)
    row = lax.broadcasted_iota(jnp.int32, (16, 64), 0)
    pitch = lax.broadcasted_iota(jnp.int32, (16, 64), 1)
    chosen = lax.rem(pitch, 16) == lax.rem(row, 8) * 2 + row // 8
    mask_e = chosen.astype(F32)
    mask_p = (chosen & (pitch < 63)).astype(F32)
    quarter_of = (
        lax.broadcasted_iota(jnp.int32, (64, 128), 0) // 16
        == lax.broadcasted_iota(jnp.int32, (64, 128), 1) // 32
    ).astype(F32)
    sub = lax.broadcasted_iota(jnp.int32, (8, 64), 0)

    def spread(rates, mask):
        wide = (rates[:, None, :] * mask[None]).reshape(128, 64)
        return jnp.dot(
            wide, quarter_of, precision=lax.Precision.HIGHEST, preferred_element_type=F32
        )

    def coefficients(b, _):
        at = pl.ds(pl.multiple_of(b * 8, 8), 8)
        along_e = spread(jnp.where(b * 8 + sub < 127, er_rows[at, :], 0.0), mask_e)
        along_p = spread(pr_rows[at, :], mask_p)
        for a in range(2):
            coef_e[a][at] = (along_e * levels[a]).reshape(8, 2, 8, 128)
            coef_p[a][at] = (along_p * levels[a]).reshape(8, 2, 8, 128)
        return 0

    lax.fori_loop(0, 16, coefficients, 0)
    zero_row = jnp.zeros((2, 8, 128), F32)
    field[0][128] = zero_row
    field[1][128] = zero_row
    other[128] = zero_row

    lanes = [lax.broadcasted_iota(jnp.int32, (n, 8, 128), 2) for n in (1, 2)]
    masks = [(lane < 64, lax.rem(lane, 64) < 32) for lane in lanes]

    def interpolate(rows, t):
        high, low = split(rows)
        both = jnp.dot(
            jnp.concatenate([high, low], axis=1), wprep[t], preferred_element_type=F32
        )
        return both[:, 0:128] + both[:, 128:256]

    def send_on(c, a, place, target):
        e, q, n = FIRST[c]
        pltpu.make_async_remote_copy(
            gath[c][a].at[place],
            field[a].at[i * 4 + e, pl.ds(q, n)],
            s_c.at[c, a],
            r_c.at[a],
            device_id=(s, target),
            device_id_type=MESH,
        ).start()

    partner = i + 1 - 2 * lax.rem(i, 2)

    def first_drift(c):
        e, q, n = FIRST[c]
        pltpu.make_async_copy(
            recv1[c].at[pl.ds(0, 21)], recv1[c].at[pl.ds(0, 21)], r_a.at[c]
        ).wait()
        for step in range(16):
            t = lax.rem(i // 2 + 3 * (step + 1), 16)
            moved = interpolate(recv1[c][slot_ref[t]], t).reshape(n, 4, 8, 128)
            outs = turn([moved[:, quarter] for quarter in range(4)], *masks[n - 1])
            if step < 15:
                for half in range(2):
                    for a in range(2):
                        gath[c][a][step * 2 + half] = outs[half * 2 + a]
                    send_on(c, 0, step * 2 + half, t * 2 + half)
            else:
                odd = lax.rem(i, 2) == 1
                for a in range(2):
                    field[a][i * 4 + e, q : q + n] = jnp.where(odd, outs[2 + a], outs[a])
                    gath[c][a][30] = jnp.where(odd, outs[a], outs[2 + a])
                send_on(c, 0, 30, partner)

    def send_rest(c, begin=0, end=16):
        def one(step, _):
            t = lax.rem(i // 2 + 3 * (step + 1), 16)
            for half in range(2):
                send_on(c, 1, step * 2 + half, t * 2 + half)
            return 0

        lax.fori_loop(begin, min(end, 15), one, 0)
        if end == 16:
            send_on(c, 1, 30, partner)

    first_drift(0)
    send_rest(0)
    first_drift(1)
    send_rest(1)
    first_drift(2)
    send_rest(2, 0, 8)
    first_drift(3)
    send_rest(2, 8, 16)
    first_drift(4)
    send_rest(3)
    send_rest(4)

    sublane = lax.broadcasted_iota(jnp.int32, (8, 128), 0)
    top, bottom = sublane == 0, sublane == 7

    def one_pass(source, target, along_e, along_p):
        def rows(b, carry):
            now, flux_before = carry
            for k in range(32):
                e = b * 32 + k
                later = source[e + 1]
                flux = along_e[e] * (later - now)
                shifted = pltpu.roll(now[0], 7, 0)
                shifted = jnp.where(bottom, pltpu.roll(shifted, 96, 1), shifted)
                pitch_low = along_p[e, 0] * (now[1] - now[0])
                pitch_high = along_p[e, 1] * (shifted - now[1])
                wrapped = pltpu.roll(pitch_high, 1, 0)
                wrapped = jnp.where(top, pltpu.roll(wrapped, 32, 1), wrapped)
                target[e, 0] = now[0] + ((flux[0] - flux_before[0]) + (pitch_low - wrapped))
                target[e, 1] = now[1] + ((flux[1] - flux_before[1]) + (pitch_high - pitch_low))
                now, flux_before = later, flux
            return now, flux_before

        lax.fori_loop(0, 4, rows, (source[0], zero_row))

    def diffuse(a):
        pltpu.make_async_copy(
            field[a].at[pl.ds(0, 124)], field[a].at[pl.ds(0, 124)], r_c.at[a]
        ).wait()

        def two_passes(_, carry):
            one_pass(field[a], other, coef_e[a], coef_p[a])
            one_pass(other, field[a], coef_e[a], coef_p[a])
            return carry

        lax.fori_loop(0, PASSES // 2, two_passes, 0)

    def send_back(a):
        for c, (e, q, n) in enumerate(LAST[a]):
            rows = pl.ds(q, n)

            def one(k, _, c=c, e=e, rows=rows):
                target = lax.rem(i + 13 * (k + 1), 32)
                pltpu.make_async_remote_copy(
                    field[a].at[target * 4 + e, rows],
                    back[a][c].at[i],
                    s_e.at[a],
                    r_e.at[a, c],
                    device_id=(s, target),
                    device_id_type=MESH,
                ).start()
                return 0

            lax.fori_loop(0, 31, one, 0)
            back[a][c][i] = field[a][i * 4 + e, q : q + n]

    for a in range(2):
        diffuse(a)
        send_back(a)

    def pack_second(a, c):
        here = back[a][c]
        pltpu.make_async_copy(here.at[pl.ds(0, 31)], here.at[pl.ds(0, 31)], r_e.at[a, c]).wait()
        for m in range(8):
            d = sector_at(m)
            for r in range(3):
                tile = pick_ref[d * 3 + r]
                for half in range(2):
                    piece = here[tile * 2 + half]
                    if m < 7:
                        send2[a][c][m, r, half] = piece
                    else:
                        recv2[a][c][s * 3 + r, half] = piece
            if m < 7:
                pltpu.make_async_remote_copy(
                    send2[a][c].at[m],
                    recv2[a][c].at[pl.ds(s * 3, 3)],
                    s_f.at[a, c],
                    r_f.at[a, c],
                    device_id=(d, i),
                    device_id_type=MESH,
                ).start()

    def arrive(a, c):
        there = recv2[a][c]
        pltpu.make_async_copy(
            there.at[pl.ds(0, 21)], there.at[pl.ds(0, 21)], r_f.at[a, c]
        ).wait()

    def second_drift(c):
        e, q, n = LAST[1][c]
        if q == 0:
            arrive(0, e)
        arrive(1, c)
        for t in range(16):
            slot = slot_ref[t]
            first, second = recv2[0][e][slot], recv2[1][c][slot]
            outs = turn(
                [first[0, q : q + n], second[0], first[1, q : q + n], second[1]], *masks[n - 1]
            )
            rows = jnp.stack(outs, axis=1).reshape(32 * n, 128)
            moved = interpolate(rows, t)
            for quarter in range(4):
                for k in range(n):
                    at = quarter * 8 + k * 32
                    order_buf[e, t, pl.ds(quarter * 16 + q + k, 8, stride=2), :] = moved[
                        at : at + 8
                    ]
            if q + n == 2:
                out_ref[e, :, t * 128 : (t + 1) * 128] = order_buf[e, t]

    for c in range(4):
        pack_second(0, c)
    pack_second(1, 0)
    for c in range(1, 5):
        pack_second(1, c)
        second_drift(c - 1)
    second_drift(4)

    for c in range(5):
        pltpu.make_async_copy(send1[c], send1[c], s_a.at[c]).wait()
        for a in range(2):
            pltpu.make_async_copy(gath[c][a], gath[c][a], s_c.at[c, a]).wait()
    for a in range(2):
        for c in range(len(LAST[a])):
            pltpu.make_async_copy(send2[a][c], send2[a][c], s_f.at[a, c]).wait()
        pltpu.make_async_copy(
            field[a].at[pl.ds(0, 124)], field[a].at[pl.ds(0, 124)], s_e.at[a]
        ).wait()


def shards(
    density,
    source_sector,
    source_tile,
    matrix_id,
    cubic_weights,
    bin_cells,
    wave_level,
    energy_rate,
    pitch_rate,
):
    place = pl.BlockSpec(memory_space=pltpu.HBM)
    dma = pltpu.SemaphoreType.DMA

    def vmem(*shape):
        return pltpu.VMEM(shape, F32)

    return pl.pallas_call(
        kernel,
        out_shape=jax.ShapeDtypeStruct((4, 64, 2048), F32),
        in_specs=[place] * 9,
        out_specs=pl.BlockSpec(memory_space=pltpu.VMEM),
        scratch_shapes=[
            *[pltpu.SMEM((1, 8, 16), jnp.int32)] * 3,
            pltpu.SMEM((1, 32), jnp.int32),
            pltpu.SMEM((1, 32), F32),
            pltpu.SMEM((24,), jnp.int32),
            pltpu.SMEM((16,), jnp.int32),
            *[vmem(16, 64, 128)] * 4,
            vmem(4, 16, 64, 128),
            vmem(32, 128, 128),
            vmem(64, 128),
            vmem(64, 128),
            vmem(128, 64),
            vmem(128, 64),
            *[vmem(7, 3, 32 * n, 128) for _, _, n in FIRST],
            *[vmem(24, 32 * n, 128) for _, _, n in FIRST],
            *[vmem(31, n, 8, 128) for _, _, n in FIRST for _ in range(2)],
            *[vmem(129, 2, 8, 128)] * 3,
            *[vmem(128, 2, 8, 128)] * 4,
            *[vmem(32, n, 8, 128) for pieces in LAST for _, _, n in pieces],
            *[vmem(7, 3, 2, n, 8, 128) for pieces in LAST for _, _, n in pieces],
            *[vmem(24, 2, n, 8, 128) for pieces in LAST for _, _, n in pieces],
            pltpu.VMEM((16, 256, 256), BF16),
            vmem(4, 16, 64, 128),
            dma((5,)),
            dma((4,)),
            dma((3,)),
            dma((5,)),
            dma((5,)),
            dma((5, 2)),
            dma((2,)),
            dma((2,)),
            dma((2, 5)),
            dma((2, 5)),
            dma((2, 5)),
        ],
        compiler_params=pltpu.CompilerParams(
            collective_id=0, has_side_effects=True, vmem_limit_bytes=50 * 2**20
        ),
        name="ion_step",
    )(
        *[
            pltpu.with_memory_space_constraint(operand, pltpu.HBM)
            for operand in (
                source_sector,
                source_tile,
                matrix_id,
                bin_cells,
                wave_level,
                density,
                cubic_weights,
                energy_rate.T,
                pitch_rate.T,
            )
        ]
    )


def solution(mesh):
    return jax.shard_map(
        shards,
        mesh=mesh,
        in_specs=(
            P("inner", None, "sector"),
            P("inner", None, None),
            P("inner", None, None),
            P("inner", None, None),
            P(),
            P("sector", None),
            P("sector", None),
            P(),
            P(),
        ),
        out_specs=P("inner", None, "sector"),
        check_vma=False,
    )
```

```python
import jax
import jax.numpy as jnp
from jax import lax
from jax.experimental import pallas as pl
from jax.experimental.pallas import tpu as pltpu
from jax.sharding import PartitionSpec as P

PASSES = 12
STRIDE = 8
MESH = pl.DeviceIdType.MESH
FIRST = ((0, 0, 1), (0, 1, 1), (1, 0, 2), (2, 0, 2), (3, 0, 2))
LAST = (
    ((0, 0, 2), (1, 0, 2), (2, 0, 2), (3, 0, 2)),
    ((0, 0, 2), (1, 0, 2), (2, 0, 2), (3, 0, 1), (3, 1, 1)),
)
F32 = jnp.float32
BF16 = jnp.bfloat16


def split(value):
    high = value.astype(BF16)
    low = (value - high.astype(F32)).astype(BF16)
    return high, low


def turn(blocks, far, near):
    b0, b1, b2, b3 = blocks

    def exchange(low, high, first, width):
        return (
            jnp.where(first, low, pltpu.roll(high, width, 2)),
            jnp.where(first, pltpu.roll(low, 128 - width, 2), high),
        )

    b0, b2 = exchange(b0, b2, far, 64)
    b1, b3 = exchange(b1, b3, far, 64)
    b0, b1 = exchange(b0, b1, near, 32)
    b2, b3 = exchange(b2, b3, near, 32)
    return b0, b1, b2, b3


def kernel(*refs):
    refs = list(refs)

    def take(count):
        out = refs[:count]
        del refs[:count]
        return out

    (src_in, tile_in, mid_in, bins_in, wave_in, dens_in, weight_in, er_in, pr_in) = take(9)
    (out_ref,) = take(1)
    src_ref, tile_ref, mid_ref, bins_ref, wave_ref, pick_ref, slot_ref = take(7)
    natural = take(4)
    tiles, weight_ref, er_ref, pr_ref, er_rows, pr_rows = take(6)
    send1 = take(5)
    recv1 = take(5)
    gath = [take(2) for _ in range(5)]
    field = take(2)
    (other,) = take(1)
    coef_e = take(2)
    coef_p = take(2)
    coef_d = take(2)
    above, beneath = take(2)
    back = [take(len(LAST[a])) for a in range(2)]
    send2 = [take(len(LAST[a])) for a in range(2)]
    recv2 = [take(len(LAST[a])) for a in range(2)]
    wprep, order_buf = take(2)
    t_sem, d_sem, w_sem, s_a, r_a, s_c, r_c, s_e, r_e, s_f, r_f = take(11)

    s = lax.axis_index("sector")
    i = lax.axis_index("inner")

    def sector_at(m):
        return lax.rem(s + 3 * (m + 1), 8)

    barrier = pltpu.get_barrier_semaphore()
    for m in range(7):
        pl.semaphore_signal(barrier, inc=1, device_id=(sector_at(m), i), device_id_type=MESH)
    for off in range(1, 32):
        pl.semaphore_signal(
            barrier, inc=1, device_id=(s, lax.rem(i + off, 32)), device_id_type=MESH
        )

    tables = [
        pltpu.make_async_copy(a, b, t_sem.at[n])
        for n, (a, b) in enumerate(
            (
                (src_in, src_ref),
                (tile_in, tile_ref),
                (mid_in, mid_ref),
                (bins_in, bins_ref),
                (wave_in, wave_ref),
            )
        )
    ]
    for copy in tables:
        copy.start()
    for e in range(4):
        for t in range(16):
            pltpu.make_async_copy(
                dens_in.at[e, :, t * 128 : (t + 1) * 128], natural[e].at[t], d_sem.at[e]
            ).start()
    parameters = [
        pltpu.make_async_copy(a, b, w_sem.at[n])
        for n, (a, b) in enumerate(
            ((weight_in, weight_ref), (er_in, er_ref), (pr_in, pr_ref))
        )
    ]
    for copy in parameters:
        copy.start()
    for copy in tables:
        copy.wait()

    for d in range(8):
        count = jnp.int32(0)
        picks = [jnp.int32(0)] * 3
        for t in range(16):
            hit = src_ref[0, d, t] == s
            tile = tile_ref[0, d, t]
            for r in range(3):
                picks[r] = jnp.where(hit & (count == r), tile, picks[r])
            count = count + hit.astype(jnp.int32)
        for r in range(3):
            pick_ref[d * 3 + r] = picks[r]

    def pack_energy(e):
        pltpu.make_async_copy(natural[e], natural[e], d_sem.at[e]).wait()
        for t in range(16):
            for quarter in range(4):
                for q in range(2):
                    to = quarter * 8 + q * 32
                    tiles[e, t, to : to + 8, :] = natural[e][
                        t, pl.ds(quarter * 16 + q, 8, stride=2), :
                    ]

    def pack_first(c):
        e, q, n = FIRST[c]
        for m in range(8):
            for r in range(3):
                block = tiles[e, pick_ref[sector_at(m) * 3 + r], 32 * q : 32 * (q + n), :]
                if m < 7:
                    send1[c][m, r] = block
                else:
                    recv1[c][s * 3 + r] = block

    def send_first(c):
        def one(m, _):
            pltpu.make_async_remote_copy(
                send1[c].at[m],
                recv1[c].at[pl.ds(s * 3, 3)],
                s_a.at[c],
                r_a.at[c],
                device_id=(sector_at(m), i),
                device_id_type=MESH,
            ).start()
            return 0

        lax.fori_loop(0, 7, one, 0)

    pack_energy(0)
    pack_first(0)
    pl.semaphore_wait(barrier, 38)
    send_first(0)
    pack_first(1)
    send_first(1)
    for c in range(2, 5):
        pack_energy(FIRST[c][0])
        pack_first(c)
        send_first(c)

    own = [src_ref[0, s, t] for t in range(16)]
    for t in range(16):
        rank = jnp.int32(0)
        for u in range(t):
            rank = rank + (own[u] == own[t]).astype(jnp.int32)
        slot_ref[t] = own[t] * 3 + rank

    for copy in parameters:
        copy.wait()
    for t in range(16):
        high, low = split(weight_ref[mid_ref[0, s, t]].T)
        wprep[t, 0:128, 0:128] = high
        wprep[t, 128:256, 0:128] = high
        wprep[t, 0:128, 128:256] = low
        wprep[t, 128:256, 128:256] = low

    er_rows[...] = er_ref[...].T
    pr_rows[...] = pr_ref[...].T
    lane_row = lax.broadcasted_iota(jnp.int32, (1, 128), 1)
    levels = []
    for a in range(2):
        cell = i * 64 + a * 32 + lax.rem(lane_row, 32)
        level = jnp.zeros((1, 128), F32)
        start = jnp.int32(0)
        for k in range(32):
            level = jnp.where(cell >= start, wave_ref[0, k], level)
            start = start + bins_ref[0, k]
        levels.append(level)
    row = lax.broadcasted_iota(jnp.int32, (16, 64), 0)
    pitch = lax.broadcasted_iota(jnp.int32, (16, 64), 1)
    chosen = lax.rem(pitch, 16) == lax.rem(row, 8) * 2 + row // 8
    mask_e = chosen.astype(F32)
    mask_p = (chosen & (pitch < 63)).astype(F32)
    quarter_of = (
        lax.broadcasted_iota(jnp.int32, (64, 128), 0) // 16
        == lax.broadcasted_iota(jnp.int32, (64, 128), 1) // 32
    ).astype(F32)
    sub = lax.broadcasted_iota(jnp.int32, (8, 64), 0)

    def spread(rates, mask):
        wide = (rates[:, None, :] * mask[None]).reshape(128, 64)
        return jnp.dot(
            wide, quarter_of, precision=lax.Precision.HIGHEST, preferred_element_type=F32
        )

    sublane = lax.broadcasted_iota(jnp.int32, (8, 128), 0)
    top, bottom = sublane == 0, sublane == 7

    def from_above(block):
        block = pltpu.roll(block, 7, 0)
        return jnp.where(bottom, pltpu.roll(block, 96, 1), block)

    def from_below(block):
        block = pltpu.roll(block, 1, 0)
        return jnp.where(top, pltpu.roll(block, 32, 1), block)

    def coefficients(b, _):
        at = pl.ds(pl.multiple_of(b * 8, 8), 8)
        along_e = spread(jnp.where(b * 8 + sub < 127, er_rows[at, :], 0.0), mask_e)
        along_p = spread(pr_rows[at, :], mask_p)
        for a in range(2):
            coef_e[a][at] = (along_e * levels[a]).reshape(8, 2, 8, 128)
            scaled = (along_p * levels[a]).reshape(8, 2, 8, 128)
            coef_p[a][at] = scaled
            for k in range(8):
                coef_d[a][b * 8 + k] = from_below(scaled[k, 1])
        return 0

    lax.fori_loop(0, 16, coefficients, 0)
    zero_row = jnp.zeros((2, 8, 128), F32)
    field[0][128] = zero_row
    field[1][128] = zero_row
    other[128] = zero_row

    lanes = [lax.broadcasted_iota(jnp.int32, (n, 8, 128), 2) for n in (1, 2)]
    masks = [(lane < 64, lax.rem(lane, 64) < 32) for lane in lanes]

    def interpolate(rows, t):
        high, low = split(rows)
        both = jnp.dot(
            jnp.concatenate([high, low], axis=1), wprep[t], preferred_element_type=F32
        )
        return both[:, 0:128] + both[:, 128:256]

    def send_on(c, a, place, target):
        e, q, n = FIRST[c]
        pltpu.make_async_remote_copy(
            gath[c][a].at[place],
            field[a].at[i * 4 + e, pl.ds(q, n)],
            s_c.at[c, a],
            r_c.at[a],
            device_id=(s, target),
            device_id_type=MESH,
        ).start()

    partner = i + 1 - 2 * lax.rem(i, 2)

    def first_drift(c):
        e, q, n = FIRST[c]
        pltpu.make_async_copy(
            recv1[c].at[pl.ds(0, 21)], recv1[c].at[pl.ds(0, 21)], r_a.at[c]
        ).wait()
        for step in range(16):
            t = lax.rem(i // 2 + 3 * (step + 1), 16)
            moved = interpolate(recv1[c][slot_ref[t]], t).reshape(n, 4, 8, 128)
            outs = turn([moved[:, quarter] for quarter in range(4)], *masks[n - 1])
            if step < 15:
                for half in range(2):
                    for a in range(2):
                        gath[c][a][step * 2 + half] = outs[half * 2 + a]
                    send_on(c, 0, step * 2 + half, t * 2 + half)
            else:
                odd = lax.rem(i, 2) == 1
                for a in range(2):
                    field[a][i * 4 + e, q : q + n] = jnp.where(odd, outs[2 + a], outs[a])
                    gath[c][a][30] = jnp.where(odd, outs[a], outs[2 + a])
                send_on(c, 0, 30, partner)

    def send_rest(c, begin=0, end=16):
        def one(step, _):
            t = lax.rem(i // 2 + 3 * (step + 1), 16)
            for half in range(2):
                send_on(c, 1, step * 2 + half, t * 2 + half)
            return 0

        lax.fori_loop(begin, min(end, 15), one, 0)
        if end == 16:
            send_on(c, 1, 30, partner)

    first_drift(0)
    send_rest(0)
    first_drift(1)
    send_rest(1)
    first_drift(2)
    send_rest(2, 0, 8)
    first_drift(3)
    first_drift(4)
    send_rest(2, 8, 16)
    send_rest(3)
    send_rest(4)

    def neighbours(ref, base, shift):
        for k in range(shift, shift + STRIDE):
            above[base + k] = from_above(ref[base + k, 0])
            beneath[base + k] = from_below(ref[base + k, 1])

    def advance(source, target, a, base, carry):
        now, flux_before = carry
        for k in range(STRIDE):
            e = base + k
            later = source[e + 1]
            flux = coef_e[a][e] * (later - now)
            low = coef_p[a][e, 0] * (now[1] - now[0])
            high = coef_p[a][e, 1] * (above[e] - now[1])
            under = coef_d[a][e] * (now[0] - beneath[e])
            target[e, 0] = now[0] + ((flux[0] - flux_before[0]) + (low - under))
            target[e, 1] = now[1] + ((flux[1] - flux_before[1]) + (high - low))
            now, flux_before = later, flux
        return now, flux_before

    def one_pass(source, target, a):
        carry = (source[0], zero_row)
        for base in range(0, 128, STRIDE):
            if base + STRIDE < 128:
                neighbours(source, base, STRIDE)
            else:
                neighbours(target, 0, 0)
            carry = advance(source, target, a, base, carry)

    def diffuse(a):
        pltpu.make_async_copy(
            field[a].at[pl.ds(0, 124)], field[a].at[pl.ds(0, 124)], r_c.at[a]
        ).wait()

        neighbours(field[a], 0, 0)

        def two_passes(_, carry):
            one_pass(field[a], other, a)
            one_pass(other, field[a], a)
            return carry

        lax.fori_loop(0, PASSES // 2, two_passes, 0)

    def send_back(a):
        for c, (e, q, n) in enumerate(LAST[a]):
            rows = pl.ds(q, n)

            def one(k, _, c=c, e=e, rows=rows):
                target = lax.rem(i + 13 * (k + 1), 32)
                pltpu.make_async_remote_copy(
                    field[a].at[target * 4 + e, rows],
                    back[a][c].at[i],
                    s_e.at[a],
                    r_e.at[a, c],
                    device_id=(s, target),
                    device_id_type=MESH,
                ).start()
                return 0

            lax.fori_loop(0, 31, one, 0)
            back[a][c][i] = field[a][i * 4 + e, q : q + n]

    for a in range(2):
        diffuse(a)
        send_back(a)

    def pack_second(a, c):
        here = back[a][c]
        pltpu.make_async_copy(here.at[pl.ds(0, 31)], here.at[pl.ds(0, 31)], r_e.at[a, c]).wait()
        for m in range(8):
            d = sector_at(m)
            for r in range(3):
                tile = pick_ref[d * 3 + r]
                for half in range(2):
                    piece = here[tile * 2 + half]
                    if m < 7:
                        send2[a][c][m, r, half] = piece
                    else:
                        recv2[a][c][s * 3 + r, half] = piece
            if m < 7:
                pltpu.make_async_remote_copy(
                    send2[a][c].at[m],
                    recv2[a][c].at[pl.ds(s * 3, 3)],
                    s_f.at[a, c],
                    r_f.at[a, c],
                    device_id=(d, i),
                    device_id_type=MESH,
                ).start()

    def arrive(a, c):
        there = recv2[a][c]
        pltpu.make_async_copy(
            there.at[pl.ds(0, 21)], there.at[pl.ds(0, 21)], r_f.at[a, c]
        ).wait()

    def second_drift(c):
        e, q, n = LAST[1][c]
        if q == 0:
            arrive(0, e)
        arrive(1, c)
        for t in range(16):
            slot = slot_ref[t]
            first, second = recv2[0][e][slot], recv2[1][c][slot]
            outs = turn(
                [first[0, q : q + n], second[0], first[1, q : q + n], second[1]], *masks[n - 1]
            )
            rows = jnp.stack(outs, axis=1).reshape(32 * n, 128)
            moved = interpolate(rows, t)
            for quarter in range(4):
                for k in range(n):
                    at = quarter * 8 + k * 32
                    order_buf[e, t, pl.ds(quarter * 16 + q + k, 8, stride=2), :] = moved[
                        at : at + 8
                    ]
            if q + n == 2:
                out_ref[e, :, t * 128 : (t + 1) * 128] = order_buf[e, t]

    for c in range(4):
        pack_second(0, c)
    pack_second(1, 0)
    for c in range(1, 5):
        pack_second(1, c)
        second_drift(c - 1)
    second_drift(4)

    for c in range(5):
        pltpu.make_async_copy(send1[c], send1[c], s_a.at[c]).wait()
        for a in range(2):
            pltpu.make_async_copy(gath[c][a], gath[c][a], s_c.at[c, a]).wait()
    for a in range(2):
        for c in range(len(LAST[a])):
            pltpu.make_async_copy(send2[a][c], send2[a][c], s_f.at[a, c]).wait()
        pltpu.make_async_copy(
            field[a].at[pl.ds(0, 124)], field[a].at[pl.ds(0, 124)], s_e.at[a]
        ).wait()


def shards(
    density,
    source_sector,
    source_tile,
    matrix_id,
    cubic_weights,
    bin_cells,
    wave_level,
    energy_rate,
    pitch_rate,
):
    place = pl.BlockSpec(memory_space=pltpu.HBM)
    dma = pltpu.SemaphoreType.DMA

    def vmem(*shape):
        return pltpu.VMEM(shape, F32)

    return pl.pallas_call(
        kernel,
        out_shape=jax.ShapeDtypeStruct((4, 64, 2048), F32),
        in_specs=[place] * 9,
        out_specs=pl.BlockSpec(memory_space=pltpu.VMEM),
        scratch_shapes=[
            *[pltpu.SMEM((1, 8, 16), jnp.int32)] * 3,
            pltpu.SMEM((1, 32), jnp.int32),
            pltpu.SMEM((1, 32), F32),
            pltpu.SMEM((24,), jnp.int32),
            pltpu.SMEM((16,), jnp.int32),
            *[vmem(16, 64, 128)] * 4,
            vmem(4, 16, 64, 128),
            vmem(32, 128, 128),
            vmem(64, 128),
            vmem(64, 128),
            vmem(128, 64),
            vmem(128, 64),
            *[vmem(7, 3, 32 * n, 128) for _, _, n in FIRST],
            *[vmem(24, 32 * n, 128) for _, _, n in FIRST],
            *[vmem(31, n, 8, 128) for _, _, n in FIRST for _ in range(2)],
            *[vmem(129, 2, 8, 128)] * 3,
            *[vmem(128, 2, 8, 128)] * 4,
            *[vmem(128, 8, 128)] * 4,
            *[vmem(32, n, 8, 128) for pieces in LAST for _, _, n in pieces],
            *[vmem(7, 3, 2, n, 8, 128) for pieces in LAST for _, _, n in pieces],
            *[vmem(24, 2, n, 8, 128) for pieces in LAST for _, _, n in pieces],
            pltpu.VMEM((16, 256, 256), BF16),
            vmem(4, 16, 64, 128),
            dma((5,)),
            dma((4,)),
            dma((3,)),
            dma((5,)),
            dma((5,)),
            dma((5, 2)),
            dma((2,)),
            dma((2,)),
            dma((2, 5)),
            dma((2, 5)),
            dma((2, 5)),
        ],
        compiler_params=pltpu.CompilerParams(
            collective_id=0, has_side_effects=True, vmem_limit_bytes=50 * 2**20
        ),
        name="ion_step",
    )(
        *[
            pltpu.with_memory_space_constraint(operand, pltpu.HBM)
            for operand in (
                source_sector,
                source_tile,
                matrix_id,
                bin_cells,
                wave_level,
                density,
                cubic_weights,
                energy_rate.T,
                pitch_rate.T,
            )
        ]
    )


def solution(mesh):
    return jax.shard_map(
        shards,
        mesh=mesh,
        in_specs=(
            P("inner", None, "sector"),
            P("inner", None, None),
            P("inner", None, None),
            P("inner", None, None),
            P(),
            P("sector", None),
            P("sector", None),
            P(),
            P(),
        ),
        out_specs=P("inner", None, "sector"),
        check_vma=False,
    )
```

```python
import jax
import jax.numpy as jnp
from jax import lax
from jax.experimental import pallas as pl
from jax.experimental.pallas import tpu as pltpu
from jax.sharding import PartitionSpec as P

PASSES = 12
STRIDE = 8
MESH = pl.DeviceIdType.MESH
FIRST = ((0, 0, 1), (0, 1, 1), (1, 0, 2), (2, 0, 2), (3, 0, 2))
LAST = (
    ((0, 0, 2), (1, 0, 2), (2, 0, 2), (3, 0, 2)),
    ((0, 0, 2), (1, 0, 2), (2, 0, 2), (3, 0, 1), (3, 1, 1)),
)
F32 = jnp.float32
BF16 = jnp.bfloat16


def split(value):
    high = value.astype(BF16)
    low = (value - high.astype(F32)).astype(BF16)
    return high, low


def turn(blocks, far, near):
    b0, b1, b2, b3 = blocks

    def exchange(low, high, first, width):
        return (
            jnp.where(first, low, pltpu.roll(high, width, 2)),
            jnp.where(first, pltpu.roll(low, 128 - width, 2), high),
        )

    b0, b2 = exchange(b0, b2, far, 64)
    b1, b3 = exchange(b1, b3, far, 64)
    b0, b1 = exchange(b0, b1, near, 32)
    b2, b3 = exchange(b2, b3, near, 32)
    return b0, b1, b2, b3


def kernel(*refs):
    refs = list(refs)

    def take(count):
        out = refs[:count]
        del refs[:count]
        return out

    (src_in, tile_in, mid_in, bins_in, wave_in, dens_in, weight_in, er_in, pr_in) = take(9)
    (out_ref,) = take(1)
    src_ref, tile_ref, mid_ref, bins_ref, wave_ref, pick_ref, slot_ref = take(7)
    natural = take(4)
    tiles, weight_ref, er_ref, pr_ref, er_rows, pr_rows = take(6)
    send1 = take(5)
    recv1 = take(5)
    gath = [take(2) for _ in range(5)]
    field = take(2)
    (other,) = take(1)
    coef_e = take(2)
    coef_p = take(2)
    coef_d = take(2)
    above, beneath = take(2)
    back = [take(len(LAST[a])) for a in range(2)]
    send2 = [take(len(LAST[a])) for a in range(2)]
    recv2 = [take(len(LAST[a])) for a in range(2)]
    wprep, order_buf = take(2)
    t_sem, d_sem, w_sem, s_a, r_a, s_c, r_c, s_e, r_e, s_f, r_f = take(11)

    s = lax.axis_index("sector")
    i = lax.axis_index("inner")

    def sector_at(m):
        return lax.rem(s + 3 * (m + 1), 8)

    barrier = pltpu.get_barrier_semaphore()
    for m in range(7):
        pl.semaphore_signal(barrier, inc=1, device_id=(sector_at(m), i), device_id_type=MESH)
    for off in range(1, 32):
        pl.semaphore_signal(
            barrier, inc=1, device_id=(s, lax.rem(i + off, 32)), device_id_type=MESH
        )

    tables = [
        pltpu.make_async_copy(a, b, t_sem.at[n])
        for n, (a, b) in enumerate(
            (
                (src_in, src_ref),
                (tile_in, tile_ref),
                (mid_in, mid_ref),
                (bins_in, bins_ref),
                (wave_in, wave_ref),
            )
        )
    ]
    for copy in tables:
        copy.start()
    def fetch(e):
        for t in range(16):
            pltpu.make_async_copy(
                dens_in.at[e, :, t * 128 : (t + 1) * 128], natural[e].at[t], d_sem.at[e]
            ).start()

    fetch(0)
    for copy in tables:
        copy.wait()

    for d in range(8):
        count = jnp.int32(0)
        picks = [jnp.int32(0)] * 3
        for t in range(16):
            hit = src_ref[0, d, t] == s
            tile = tile_ref[0, d, t]
            for r in range(3):
                picks[r] = jnp.where(hit & (count == r), tile, picks[r])
            count = count + hit.astype(jnp.int32)
        for r in range(3):
            pick_ref[d * 3 + r] = picks[r]

    def pack_energy(e):
        pltpu.make_async_copy(natural[e], natural[e], d_sem.at[e]).wait()
        for t in range(16):
            for quarter in range(4):
                for q in range(2):
                    to = quarter * 8 + q * 32
                    tiles[e, t, to : to + 8, :] = natural[e][
                        t, pl.ds(quarter * 16 + q, 8, stride=2), :
                    ]

    def pack_first(c):
        e, q, n = FIRST[c]
        for m in range(8):
            for r in range(3):
                block = tiles[e, pick_ref[sector_at(m) * 3 + r], 32 * q : 32 * (q + n), :]
                if m < 7:
                    send1[c][m, r] = block
                else:
                    recv1[c][s * 3 + r] = block

    def send_first(c):
        def one(m, _):
            pltpu.make_async_remote_copy(
                send1[c].at[m],
                recv1[c].at[pl.ds(s * 3, 3)],
                s_a.at[c],
                r_a.at[c],
                device_id=(sector_at(m), i),
                device_id_type=MESH,
            ).start()
            return 0

        lax.fori_loop(0, 7, one, 0)

    pack_energy(0)
    pack_first(0)
    pl.semaphore_wait(barrier, 38)
    send_first(0)
    pack_first(1)
    send_first(1)
    for e in range(1, 4):
        fetch(e)
    parameters = [
        pltpu.make_async_copy(a, b, w_sem.at[n])
        for n, (a, b) in enumerate(
            ((weight_in, weight_ref), (er_in, er_ref), (pr_in, pr_ref))
        )
    ]
    for copy in parameters:
        copy.start()
    for c in range(2, 5):
        pack_energy(FIRST[c][0])
        pack_first(c)
        send_first(c)

    own = [src_ref[0, s, t] for t in range(16)]
    for t in range(16):
        rank = jnp.int32(0)
        for u in range(t):
            rank = rank + (own[u] == own[t]).astype(jnp.int32)
        slot_ref[t] = own[t] * 3 + rank

    for copy in parameters:
        copy.wait()
    for t in range(16):
        high, low = split(weight_ref[mid_ref[0, s, t]].T)
        wprep[t, 0:128, 0:128] = high
        wprep[t, 128:256, 0:128] = high
        wprep[t, 0:128, 128:256] = low
        wprep[t, 128:256, 128:256] = low

    er_rows[...] = er_ref[...].T
    pr_rows[...] = pr_ref[...].T
    lane_row = lax.broadcasted_iota(jnp.int32, (1, 128), 1)
    levels = []
    for a in range(2):
        cell = i * 64 + a * 32 + lax.rem(lane_row, 32)
        level = jnp.zeros((1, 128), F32)
        start = jnp.int32(0)
        for k in range(32):
            level = jnp.where(cell >= start, wave_ref[0, k], level)
            start = start + bins_ref[0, k]
        levels.append(level)
    row = lax.broadcasted_iota(jnp.int32, (16, 64), 0)
    pitch = lax.broadcasted_iota(jnp.int32, (16, 64), 1)
    chosen = lax.rem(pitch, 16) == lax.rem(row, 8) * 2 + row // 8
    mask_e = chosen.astype(F32)
    mask_p = (chosen & (pitch < 63)).astype(F32)
    quarter_of = (
        lax.broadcasted_iota(jnp.int32, (64, 128), 0) // 16
        == lax.broadcasted_iota(jnp.int32, (64, 128), 1) // 32
    ).astype(F32)
    sub = lax.broadcasted_iota(jnp.int32, (8, 64), 0)

    def spread(rates, mask):
        wide = (rates[:, None, :] * mask[None]).reshape(128, 64)
        return jnp.dot(
            wide, quarter_of, precision=lax.Precision.HIGHEST, preferred_element_type=F32
        )

    sublane = lax.broadcasted_iota(jnp.int32, (8, 128), 0)
    top, bottom = sublane == 0, sublane == 7

    def from_above(block):
        block = pltpu.roll(block, 7, 0)
        return jnp.where(bottom, pltpu.roll(block, 96, 1), block)

    def from_below(block):
        block = pltpu.roll(block, 1, 0)
        return jnp.where(top, pltpu.roll(block, 32, 1), block)

    def coefficients(b, _):
        at = pl.ds(pl.multiple_of(b * 8, 8), 8)
        along_e = spread(jnp.where(b * 8 + sub < 127, er_rows[at, :], 0.0), mask_e)
        along_p = spread(pr_rows[at, :], mask_p)
        for a in range(2):
            coef_e[a][at] = (along_e * levels[a]).reshape(8, 2, 8, 128)
            scaled = (along_p * levels[a]).reshape(8, 2, 8, 128)
            coef_p[a][at] = scaled
            for k in range(8):
                coef_d[a][b * 8 + k] = from_below(scaled[k, 1])
        return 0

    lax.fori_loop(0, 16, coefficients, 0)
    zero_row = jnp.zeros((2, 8, 128), F32)
    field[0][128] = zero_row
    field[1][128] = zero_row
    other[128] = zero_row

    lanes = [lax.broadcasted_iota(jnp.int32, (n, 8, 128), 2) for n in (1, 2)]
    masks = [(lane < 64, lax.rem(lane, 64) < 32) for lane in lanes]

    def interpolate(rows, t):
        high, low = split(rows)
        both = jnp.dot(
            jnp.concatenate([high, low], axis=1), wprep[t], preferred_element_type=F32
        )
        return both[:, 0:128] + both[:, 128:256]

    def send_on(c, a, place, target):
        e, q, n = FIRST[c]
        pltpu.make_async_remote_copy(
            gath[c][a].at[place],
            field[a].at[i * 4 + e, pl.ds(q, n)],
            s_c.at[c, a],
            r_c.at[a],
            device_id=(s, target),
            device_id_type=MESH,
        ).start()

    partner = i + 1 - 2 * lax.rem(i, 2)

    def first_drift(c):
        e, q, n = FIRST[c]
        pltpu.make_async_copy(
            recv1[c].at[pl.ds(0, 21)], recv1[c].at[pl.ds(0, 21)], r_a.at[c]
        ).wait()
        for step in range(16):
            t = lax.rem(i // 2 + 3 * (step + 1), 16)
            moved = interpolate(recv1[c][slot_ref[t]], t).reshape(n, 4, 8, 128)
            outs = turn([moved[:, quarter] for quarter in range(4)], *masks[n - 1])
            if step < 15:
                for half in range(2):
                    for a in range(2):
                        gath[c][a][step * 2 + half] = outs[half * 2 + a]
                    send_on(c, 0, step * 2 + half, t * 2 + half)
            else:
                odd = lax.rem(i, 2) == 1
                for a in range(2):
                    field[a][i * 4 + e, q : q + n] = jnp.where(odd, outs[2 + a], outs[a])
                    gath[c][a][30] = jnp.where(odd, outs[a], outs[2 + a])
                send_on(c, 0, 30, partner)

    def send_rest(c, begin=0, end=16):
        def one(step, _):
            t = lax.rem(i // 2 + 3 * (step + 1), 16)
            for half in range(2):
                send_on(c, 1, step * 2 + half, t * 2 + half)
            return 0

        lax.fori_loop(begin, min(end, 15), one, 0)
        if end == 16:
            send_on(c, 1, 30, partner)

    first_drift(0)
    send_rest(0)
    first_drift(1)
    send_rest(1)
    first_drift(2)
    send_rest(2, 0, 8)
    first_drift(3)
    first_drift(4)
    send_rest(2, 8, 16)
    send_rest(3)
    send_rest(4)

    def neighbours(ref, base, shift):
        for k in range(shift, shift + STRIDE):
            above[base + k] = from_above(ref[base + k, 0])
            beneath[base + k] = from_below(ref[base + k, 1])

    def advance(source, target, a, base, carry):
        now, flux_before = carry
        for k in range(STRIDE):
            e = base + k
            later = source[e + 1]
            flux = coef_e[a][e] * (later - now)
            low = coef_p[a][e, 0] * (now[1] - now[0])
            high = coef_p[a][e, 1] * (above[e] - now[1])
            under = coef_d[a][e] * (now[0] - beneath[e])
            target[e, 0] = now[0] + ((flux[0] - flux_before[0]) + (low - under))
            target[e, 1] = now[1] + ((flux[1] - flux_before[1]) + (high - low))
            now, flux_before = later, flux
        return now, flux_before

    def one_pass(source, target, a):
        carry = (source[0], zero_row)
        for base in range(0, 128, STRIDE):
            if base + STRIDE < 128:
                neighbours(source, base, STRIDE)
            else:
                neighbours(target, 0, 0)
            carry = advance(source, target, a, base, carry)

    def diffuse(a):
        pltpu.make_async_copy(
            field[a].at[pl.ds(0, 124)], field[a].at[pl.ds(0, 124)], r_c.at[a]
        ).wait()

        neighbours(field[a], 0, 0)

        def two_passes(_, carry):
            one_pass(field[a], other, a)
            one_pass(other, field[a], a)
            return carry

        lax.fori_loop(0, PASSES // 2, two_passes, 0)

    def send_back(a):
        for c, (e, q, n) in enumerate(LAST[a]):
            rows = pl.ds(q, n)

            def one(k, _, c=c, e=e, rows=rows):
                target = lax.rem(i + 13 * (k + 1), 32)
                pltpu.make_async_remote_copy(
                    field[a].at[target * 4 + e, rows],
                    back[a][c].at[i],
                    s_e.at[a],
                    r_e.at[a, c],
                    device_id=(s, target),
                    device_id_type=MESH,
                ).start()
                return 0

            lax.fori_loop(0, 31, one, 0)
            back[a][c][i] = field[a][i * 4 + e, q : q + n]

    for a in range(2):
        diffuse(a)
        send_back(a)

    def pack_second(a, c):
        here = back[a][c]
        pltpu.make_async_copy(here.at[pl.ds(0, 31)], here.at[pl.ds(0, 31)], r_e.at[a, c]).wait()
        for m in range(8):
            d = sector_at(m)
            for r in range(3):
                tile = pick_ref[d * 3 + r]
                for half in range(2):
                    piece = here[tile * 2 + half]
                    if m < 7:
                        send2[a][c][m, r, half] = piece
                    else:
                        recv2[a][c][s * 3 + r, half] = piece
            if m < 7:
                pltpu.make_async_remote_copy(
                    send2[a][c].at[m],
                    recv2[a][c].at[pl.ds(s * 3, 3)],
                    s_f.at[a, c],
                    r_f.at[a, c],
                    device_id=(d, i),
                    device_id_type=MESH,
                ).start()

    def arrive(a, c):
        there = recv2[a][c]
        pltpu.make_async_copy(
            there.at[pl.ds(0, 21)], there.at[pl.ds(0, 21)], r_f.at[a, c]
        ).wait()

    def second_drift(c):
        e, q, n = LAST[1][c]
        if q == 0:
            arrive(0, e)
        arrive(1, c)
        for t in range(16):
            slot = slot_ref[t]
            first, second = recv2[0][e][slot], recv2[1][c][slot]
            outs = turn(
                [first[0, q : q + n], second[0], first[1, q : q + n], second[1]], *masks[n - 1]
            )
            rows = jnp.stack(outs, axis=1).reshape(32 * n, 128)
            moved = interpolate(rows, t)
            for quarter in range(4):
                for k in range(n):
                    at = quarter * 8 + k * 32
                    order_buf[e, t, pl.ds(quarter * 16 + q + k, 8, stride=2), :] = moved[
                        at : at + 8
                    ]
            if q + n == 2:
                out_ref[e, :, t * 128 : (t + 1) * 128] = order_buf[e, t]

    for c in range(4):
        pack_second(0, c)
    pack_second(1, 0)
    for c in range(1, 5):
        pack_second(1, c)
        second_drift(c - 1)
    second_drift(4)

    for c in range(5):
        pltpu.make_async_copy(send1[c], send1[c], s_a.at[c]).wait()
        for a in range(2):
            pltpu.make_async_copy(gath[c][a], gath[c][a], s_c.at[c, a]).wait()
    for a in range(2):
        for c in range(len(LAST[a])):
            pltpu.make_async_copy(send2[a][c], send2[a][c], s_f.at[a, c]).wait()
        pltpu.make_async_copy(
            field[a].at[pl.ds(0, 124)], field[a].at[pl.ds(0, 124)], s_e.at[a]
        ).wait()


def shards(
    density,
    source_sector,
    source_tile,
    matrix_id,
    cubic_weights,
    bin_cells,
    wave_level,
    energy_rate,
    pitch_rate,
):
    place = pl.BlockSpec(memory_space=pltpu.HBM)
    dma = pltpu.SemaphoreType.DMA

    def vmem(*shape):
        return pltpu.VMEM(shape, F32)

    return pl.pallas_call(
        kernel,
        out_shape=jax.ShapeDtypeStruct((4, 64, 2048), F32),
        in_specs=[place] * 9,
        out_specs=pl.BlockSpec(memory_space=pltpu.VMEM),
        scratch_shapes=[
            *[pltpu.SMEM((1, 8, 16), jnp.int32)] * 3,
            pltpu.SMEM((1, 32), jnp.int32),
            pltpu.SMEM((1, 32), F32),
            pltpu.SMEM((24,), jnp.int32),
            pltpu.SMEM((16,), jnp.int32),
            *[vmem(16, 64, 128)] * 4,
            vmem(4, 16, 64, 128),
            vmem(32, 128, 128),
            vmem(64, 128),
            vmem(64, 128),
            vmem(128, 64),
            vmem(128, 64),
            *[vmem(7, 3, 32 * n, 128) for _, _, n in FIRST],
            *[vmem(24, 32 * n, 128) for _, _, n in FIRST],
            *[vmem(31, n, 8, 128) for _, _, n in FIRST for _ in range(2)],
            *[vmem(129, 2, 8, 128)] * 3,
            *[vmem(128, 2, 8, 128)] * 4,
            *[vmem(128, 8, 128)] * 4,
            *[vmem(32, n, 8, 128) for pieces in LAST for _, _, n in pieces],
            *[vmem(7, 3, 2, n, 8, 128) for pieces in LAST for _, _, n in pieces],
            *[vmem(24, 2, n, 8, 128) for pieces in LAST for _, _, n in pieces],
            pltpu.VMEM((16, 256, 256), BF16),
            vmem(4, 16, 64, 128),
            dma((5,)),
            dma((4,)),
            dma((3,)),
            dma((5,)),
            dma((5,)),
            dma((5, 2)),
            dma((2,)),
            dma((2,)),
            dma((2, 5)),
            dma((2, 5)),
            dma((2, 5)),
        ],
        compiler_params=pltpu.CompilerParams(
            collective_id=0, has_side_effects=True, vmem_limit_bytes=50 * 2**20
        ),
        name="ion_step",
    )(
        *[
            pltpu.with_memory_space_constraint(operand, pltpu.HBM)
            for operand in (
                source_sector,
                source_tile,
                matrix_id,
                bin_cells,
                wave_level,
                density,
                cubic_weights,
                energy_rate.T,
                pitch_rate.T,
            )
        ]
    )


def solution(mesh):
    return jax.shard_map(
        shards,
        mesh=mesh,
        in_specs=(
            P("inner", None, "sector"),
            P("inner", None, None),
            P("inner", None, None),
            P("inner", None, None),
            P(),
            P("sector", None),
            P("sector", None),
            P(),
            P(),
        ),
        out_specs=P("inner", None, "sector"),
        check_vma=False,
    )
```
